32 devices in a mesh: groups: 2 (over x), tile: 16 (over z, y, core).
Axes of the slice: x: 2, y: 2, z: 4, core: 2. Of those that a mesh axis runs over, the one named last changes fastest.
Arguments:
- fine_nodes: bfloat16 [32768, 512], P(('groups', 'tile')), parts along dimension 0, may hold values from -6 to 6
- fine_table: int32 [16384, 6], P('tile'), may hold values from 0 to 16383, as said below
- mid_table: int32 [4096, 6], P('tile'), may hold values from 0 to 4095, as said below
- coarse_table: int32 [1024, 6], replicated, may hold values from 0 to 1023, as said below
- fine_parent: int32 [16384], P('tile'), may hold values from 0 to 4095, as said below
- mid_parent: int32 [4096], P('tile'), may hold values from 0 to 1023, as said below
- edge_self: bfloat16 [3, 512, 512], replicated, may hold values from -0.1875 to 0.1875
- edge_peer: bfloat16 [3, 512, 512], replicated, may hold values from -0.1875 to 0.1875
- edge_bias: float32 [3, 512], replicated, may hold values from -3 to 3
- node_self: bfloat16 [3, 512, 512], replicated, may hold values from -0.1875 to 0.1875
- node_message: bfloat16 [3, 512, 512], replicated, may hold values from -0.109375 to 0.109375
- node_bias: float32 [3, 512], replicated, may hold values from -3 to 3
- node_out: bfloat16 [3, 512, 512], replicated, may hold values from -0.25 to 0.25
- ascend_gain: float32 [2, 512], replicated, may hold values from 0.1 to 1.9
- down_self: bfloat16 [2, 512, 512], replicated, may hold values from -0.1875 to 0.1875
- down_parent: bfloat16 [2, 512, 512], replicated, may hold values from -0.1875 to 0.1875
- down_bias: float32 [2, 512], replicated, may hold values from -3 to 3
- down_out: bfloat16 [2, 512, 512], replicated, may hold values from -0.25 to 0.25
Outputs:
- fine_out: bfloat16 [32768, 512], P(('groups', 'tile')), parts along dimension 0
- mid_out: bfloat16 [8192, 512], P(('groups', 'tile')), parts along dimension 0
- coarse_out: bfloat16 [2048, 512], P(('groups', 'tile')), parts along dimension 0
The draws below stay inside these ranges and needn't reach their ends.
There are 2 independent parts, one for each index of `groups`. The reference program is written for one: setup_inputs(seed, part) draws one part's arguments, and reference() takes and returns one part's arrays. A program takes and returns all parts, laid end to end along the dimension named above; an argument that names none is the same for every part. Nothing has to cross between parts.
Inputs may be any that keep to these rules, and one draw needn't show every extreme that they name: `fine_table`: fine node n is grid cell (n // 256, n % 256); each of its six neighbours lies in its own grid row or one of the two rows beside it, columns wrapping around. `mid_table`: Level-1 node p is cell (p // 128, p % 128); each neighbour lies in its own row or one of the two rows beside it, columns wrapping around. `coarse_table`: any level-2 nodes. `fine_parent`: the parent of fine cell (r, c) lies in level-1 row r // 2 - 1, r // 2 or r // 2 + 1. `mid_parent`: the parent of level-1 cell (r, c) lies in level-2 row r // 2 - 1, r // 2 or r // 2 + 1.
All inputs are finite; a program needn't handle non-finite values.
Results may differ from the reference program's by a relative error of at most 0.014.
Values may be sent and summed in bfloat16 or wider, within the bound.
A program may use at most 64 MiB of HBM per device.

```python
import jax
import jax.numpy as jnp
import numpy as np
from jax import lax

D = 512
COLS = 256
ROWS = 64
NODES0 = 16384
ROWS1 = 32
COLS1 = 128
NODES1 = 4096
NODES2 = 1024


def grid_neighbours(base_key, row_total, col_total):
    cell_ids = jnp.arange(row_total * col_total, dtype=jnp.int32)
    row_of = cell_ids // col_total
    col_of = cell_ids % col_total
    row_step = jnp.array(np.array([0, 0, 1, -1, 1, -1], np.int32))
    col_step = jnp.array(np.array([1, -1, 0, 0, -1, 1], np.int32))
    jitter = jax.random.randint(base_key, (row_total * col_total, 6), -2, 3, dtype=jnp.int32)
    near_row = jnp.clip(row_of[:, None] + row_step[None, :], 0, row_total - 1)
    near_col = (col_of[:, None] + col_step[None, :] + jitter) % col_total
    return (near_row * col_total + near_col).astype(jnp.int32)


def grid_parents(base_key, row_total, col_total):
    cell_ids = jnp.arange(row_total * col_total, dtype=jnp.int32)
    row_of = cell_ids // col_total
    col_of = cell_ids % col_total
    first_key, second_key = jax.random.split(base_key)
    row_move = jax.random.randint(first_key, (row_total * col_total,), -1, 2, dtype=jnp.int32)
    col_move = jax.random.randint(second_key, (row_total * col_total,), -1, 2, dtype=jnp.int32)
    upper_rows = row_total // 2
    upper_cols = col_total // 2
    parent_row = jnp.clip(row_of // 2 + row_move, 0, upper_rows - 1)
    parent_col = (col_of // 2 + col_move) % upper_cols
    return (parent_row * upper_cols + parent_col).astype(jnp.int32)


def draw_fine_table(key, part):
    return grid_neighbours(jax.random.fold_in(key, 11), ROWS, COLS)


def draw_mid_table(key, part):
    return grid_neighbours(jax.random.fold_in(key, 12), ROWS1, COLS1)


def draw_coarse_table(key, part):
    return jax.random.randint(jax.random.fold_in(key, 13), (NODES2, 6), 0, NODES2, dtype=jnp.int32)


def draw_fine_parent(key, part):
    return grid_parents(jax.random.fold_in(key, 14), ROWS, COLS)


def draw_mid_parent(key, part):
    return grid_parents(jax.random.fold_in(key, 15), ROWS1, COLS1)


def shard_levels(own_key, dims, cuts, low, top_value):
    level, own = 1.0, jax.random.fold_in(own_key, 6)
    for position, blocks in cuts:
        draws = jnp.exp(jax.random.uniform(jax.random.fold_in(own, position), (blocks,), jnp.float32, low / len(cuts), top_value / len(cuts)))
        level = level * jnp.repeat(draws, dims[position] // blocks).reshape([-1 if axis == position else 1 for axis in range(len(dims))])
    return level


def noise(own_key, dims, spread, most, pieces=(), kind=jnp.bfloat16):
    drawn = spread * jax.random.normal(own_key, dims, jnp.float32)
    if pieces:
        drawn = drawn * shard_levels(own_key, dims, pieces, -0.22, 0.18)
    return jnp.clip(drawn, -most, most).astype(kind)


def setup_inputs(seed: int = 0, part: int = 0) -> dict:
    splits = jax.random.split(jax.random.key(seed), 19)
    own_keys = jax.random.split(jax.random.fold_in(splits[18], part), 19)
    fine_nodes = noise(own_keys[0], (NODES0, D), 1.0, 6.0, ((0, 16),))
    fine_table = draw_fine_table(jax.random.fold_in(splits[18], 71), part)
    mid_table = draw_mid_table(jax.random.fold_in(splits[18], 71), part)
    coarse_table = draw_coarse_table(jax.random.fold_in(splits[18], 71), part)
    fine_parent = draw_fine_parent(jax.random.fold_in(splits[18], 71), part)
    mid_parent = draw_mid_parent(jax.random.fold_in(splits[18], 71), part)
    edge_self = noise(splits[6], (3, D, D), (2 * D) ** -0.5, 0.1875)
    edge_peer = noise(splits[7], (3, D, D), (2 * D) ** -0.5, 0.1875)
    edge_bias = noise(splits[8], (3, D), 0.5, 3.0, (), jnp.float32)
    node_self = noise(splits[9], (3, D, D), (2 * D) ** -0.5, 0.1875)
    node_message = noise(splits[10], (3, D, D), (6 * D) ** -0.5, 0.109375)
    node_bias = noise(splits[11], (3, D), 0.5, 3.0, (), jnp.float32)
    node_out = noise(splits[12], (3, D, D), D ** -0.5, 0.25)
    ascend_gain = jnp.clip(1.0 + 0.18 * jax.random.normal(splits[13], (2, D), jnp.float32), 0.1, 1.9)
    down_self = noise(splits[14], (2, D, D), (2 * D) ** -0.5, 0.1875)
    down_parent = noise(splits[15], (2, D, D), (2 * D) ** -0.5, 0.1875)
    down_bias = noise(splits[16], (2, D), 0.5, 3.0, (), jnp.float32)
    down_out = noise(splits[17], (2, D, D), D ** -0.5, 0.25)
    return dict(fine_nodes=fine_nodes, fine_table=fine_table, mid_table=mid_table, coarse_table=coarse_table, fine_parent=fine_parent, mid_parent=mid_parent, edge_self=edge_self, edge_peer=edge_peer, edge_bias=edge_bias, node_self=node_self, node_message=node_message, node_bias=node_bias, node_out=node_out, ascend_gain=ascend_gain, down_self=down_self, down_parent=down_parent, down_bias=down_bias, down_out=down_out)


def gelu_tanh(values):
    return jax.nn.gelu(values, approximate=True)

def process_level(node_rows, neighbours, level_index, weights):
    edge_self, edge_peer, edge_bias, node_self, node_message, node_bias, node_out = weights
    own_proj = jnp.dot(node_rows, edge_self[level_index], preferred_element_type=jnp.float32) + edge_bias[level_index]
    peer_proj = jnp.dot(node_rows, edge_peer[level_index], preferred_element_type=jnp.float32).astype(jnp.bfloat16)
    summed = jnp.zeros(own_proj.shape, jnp.float32)
    for slot_index in range(6):
        fetched = jnp.take(peer_proj, neighbours[:, slot_index], axis=0).astype(jnp.float32)
        summed = summed + gelu_tanh(own_proj + fetched)
    message = summed.astype(jnp.bfloat16)
    pre_act = jnp.dot(node_rows, node_self[level_index], preferred_element_type=jnp.float32)
    pre_act = pre_act + jnp.dot(message, node_message[level_index], preferred_element_type=jnp.float32) + node_bias[level_index]
    hidden = gelu_tanh(pre_act).astype(jnp.bfloat16)
    result = node_rows.astype(jnp.float32) + jnp.dot(hidden, node_out[level_index], preferred_element_type=jnp.float32)
    return result.astype(jnp.bfloat16)

def ascend_level(children, parents, parent_count, gain_vec):
    summed = jax.ops.segment_sum(children.astype(jnp.float32), parents, num_segments=parent_count)
    scale_inv = lax.rsqrt(lax.optimization_barrier(jnp.mean(summed * summed, axis=1, keepdims=True)) + 1e-05)
    return (summed * scale_inv * gain_vec).astype(jnp.bfloat16)

def descend_level(children, parent_rows, parents, level_index, downs):
    down_self, down_parent, down_bias, down_out = downs
    lifted = jnp.dot(parent_rows, down_parent[level_index], preferred_element_type=jnp.float32).astype(jnp.bfloat16)
    pre_act = jnp.dot(children, down_self[level_index], preferred_element_type=jnp.float32)
    pre_act = pre_act + jnp.take(lifted, parents, axis=0).astype(jnp.float32) + down_bias[level_index]
    hidden = gelu_tanh(pre_act).astype(jnp.bfloat16)
    result = children.astype(jnp.float32) + jnp.dot(hidden, down_out[level_index], preferred_element_type=jnp.float32)
    return result.astype(jnp.bfloat16)

def reference(fine_nodes, fine_table, mid_table, coarse_table, fine_parent, mid_parent, edge_self, edge_peer, edge_bias, node_self, node_message, node_bias, node_out, ascend_gain, down_self, down_parent, down_bias, down_out):
    weights = (edge_self, edge_peer, edge_bias, node_self, node_message, node_bias, node_out)
    downs = (down_self, down_parent, down_bias, down_out)
    fine_rows = process_level(fine_nodes, fine_table, 0, weights)
    mid_start = ascend_level(fine_rows, fine_parent, NODES1, ascend_gain[0])
    mid_rows = process_level(mid_start, mid_table, 1, weights)
    coarse_start = ascend_level(mid_rows, mid_parent, NODES2, ascend_gain[1])
    coarse_rows = process_level(coarse_start, coarse_table, 2, weights)
    mid_final = descend_level(mid_rows, coarse_rows, mid_parent, 1, downs)
    fine_final = descend_level(fine_rows, mid_final, fine_parent, 0, downs)
    return (fine_final, mid_final, coarse_rows)
```

```python
import functools

import jax
import jax.numpy as jnp
from jax import lax
from jax.experimental import pallas as pl
from jax.experimental.pallas import tpu as pltpu
from jax.sharding import PartitionSpec as P

COLS = 256
BF = jnp.bfloat16
F32 = jnp.float32


def gelu(v):
    inner = v * (0.7978845608028654 + (0.7978845608028654 * 0.044715) * (v * v))
    half = 0.5 * v
    return half + half * jnp.tanh(inner)


def mm(a, b):
    return jnp.dot(a, b, preferred_element_type=F32)


def onehot_cols(ids, width):
    lanes = lax.broadcasted_iota(jnp.int32, (ids.shape[0], width), 1)
    return jnp.where(lanes == ids, 1.0, 0.0).astype(BF)


def onehot_rows(ids, height):
    rows = lax.broadcasted_iota(jnp.int32, (height, ids.shape[1]), 0)
    return jnp.where(rows == ids, 1.0, 0.0).astype(BF)


def sweep(
    n,
    span_y,
    cols0,
    x_hbm,
    col0_ref,
    col1_ref,
    ctab_ref,
    par0_ref,
    par1_ref,
    edge_self_hbm,
    edge_peer_hbm,
    node_self_hbm,
    node_message_hbm,
    node_out_hbm,
    down_self_hbm,
    down_parent_hbm,
    down_out_hbm,
    edge_bias_ref,
    node_bias_ref,
    gain_ref,
    down_bias_ref,
    fine_out,
    mid_out,
    coarse_out,
    x,
    edge_self,
    edge_peer,
    node_self,
    node_message,
    node_out,
    down_self,
    down_parent,
    down_out,
    ext0,
    fine,
    pre0,
    send1,
    recv1,
    ext1,
    mid,
    pre1,
    send2,
    recv2,
    gath,
    extc,
    extl,
    load_sem,
    send_sem,
    recv_sem,
    gsend_z,
    gsend_y,
    gsend_c,
    grecv,
):
    me = lax.axis_index("tile")
    n0, d = x.shape
    rows0 = n0 // cols0
    c1 = cols0 // 2
    n1 = mid.shape[0]
    n2 = coarse_out.shape[0]
    c2 = n2
    has_left = me > 0
    has_right = me < n - 1
    left = jnp.maximum(me - 1, 0)
    right = jnp.minimum(me + 1, n - 1)

    loads = {}
    slot = 0

    def load(name, src, dst):
        nonlocal slot
        cp = pltpu.make_async_copy(src, dst, load_sem.at[slot])
        cp.start()
        loads[name] = cp
        slot += 1

    load("x", x_hbm, x)
    load(("edge_peer", 0), edge_peer_hbm.at[0], edge_peer.at[0])
    load(("edge_self", 0), edge_self_hbm.at[0], edge_self.at[0])
    load(("node_self", 0), node_self_hbm.at[0], node_self.at[0])
    load(("node_message", 0), node_message_hbm.at[0], node_message.at[0])
    load(("node_out", 0), node_out_hbm.at[0], node_out.at[0])
    for lv in (1, 2):
        load(("edge_peer", lv), edge_peer_hbm.at[lv], edge_peer.at[lv])
        load(("edge_self", lv), edge_self_hbm.at[lv], edge_self.at[lv])
        load(("node_self", lv), node_self_hbm.at[lv], node_self.at[lv])
        load(("node_message", lv), node_message_hbm.at[lv], node_message.at[lv])
        load(("node_out", lv), node_out_hbm.at[lv], node_out.at[lv])
    load("down_self", down_self_hbm, down_self)
    load("down_parent", down_parent_hbm, down_parent)
    load("down_out", down_out_hbm, down_out)

    span_z = n // (2 * span_y)
    core = me % 2
    yy = (me // 2) % span_y
    zz = me // (2 * span_y)

    def tile_of(z, y, c):
        return (z * span_y + y) * 2 + c

    def zother(k):
        out = 0
        bit = 1
        while bit < span_z:
            mine = (zz // bit) % 2
            out = out + (1 - mine if k & bit else mine) * bit
            bit *= 2
        return out

    z_partners = [zother(k) for k in range(1, span_z)]
    y_other = 1 - yy if span_y == 2 else None
    c_other = 1 - core

    barrier = pltpu.get_barrier_semaphore()

    @pl.when(has_left)
    def _():
        pl.semaphore_signal(barrier, inc=1, device_id={"tile": left})

    @pl.when(has_right)
    def _():
        pl.semaphore_signal(barrier, inc=1, device_id={"tile": right})

    partners = [tile_of(z, yy, core) for z in z_partners]
    if span_y == 2:
        partners.append(tile_of(zz, y_other, core))
    partners.append(tile_of(zz, yy, c_other))
    for p in partners:
        pl.semaphore_signal(barrier, inc=1, device_id={"tile": p})

    def halo(e, low, low_dst, high, high_dst):
        to_left = pltpu.make_async_remote_copy(
            src_ref=low,
            dst_ref=low_dst,
            send_sem=send_sem.at[2 * e],
            recv_sem=recv_sem.at[2 * e + 1],
            device_id={"tile": left},
        )
        to_right = pltpu.make_async_remote_copy(
            src_ref=high,
            dst_ref=high_dst,
            send_sem=send_sem.at[2 * e + 1],
            recv_sem=recv_sem.at[2 * e],
            device_id={"tile": right},
        )
        return to_left, to_right

    def send_left(h):
        @pl.when(has_left)
        def _():
            h[0].start()

    def send_right(h):
        @pl.when(has_right)
        def _():
            h[1].start()

    def wait_left(h):
        @pl.when(has_left)
        def _():
            h[1].wait_recv()

    def wait_right(h):
        @pl.when(has_right)
        def _():
            h[0].wait_recv()

    def drain(h):
        @pl.when(has_left)
        def _():
            h[0].wait_send()

        @pl.when(has_right)
        def _():
            h[1].wait_send()

    def zero_edges(low, high):
        @pl.when(me == 0)
        def _():
            low[...] = jnp.zeros(low.shape, low.dtype)

        @pl.when(me == n - 1)
        def _():
            high[...] = jnp.zeros(high.shape, high.dtype)

    zero_edges(ext0.at[pl.ds(0, cols0)], ext0.at[pl.ds(n0 + cols0, cols0)])
    zero_edges(recv1.at[0], recv1.at[1])
    zero_edges(ext1.at[pl.ds(0, c1)], ext1.at[pl.ds(n1 + c1, c1)])
    zero_edges(recv2.at[0], recv2.at[1])
    zero_edges(extc.at[pl.ds(0, c2)], extc.at[pl.ds(n2 + c2, c2)])
    zero_edges(extl.at[pl.ds(0, c1)], extl.at[pl.ds(n1 + c1, c1)])

    loads["x"].wait()
    loads[("edge_peer", 0)].wait()

    def peer_row(r):
        at = pl.multiple_of(r * cols0, cols0)
        ext0[pl.ds(pl.multiple_of(at + cols0, cols0), cols0), :] = mm(
            x[pl.ds(at, cols0), :], edge_peer[0]
        ).astype(BF)

    peer_row(0)
    peer_row(rows0 - 1)
    pl.semaphore_wait(barrier, len(partners) + has_left.astype(jnp.int32) + has_right.astype(jnp.int32))
    h0 = halo(
        0,
        ext0.at[pl.ds(cols0, cols0)],
        ext0.at[pl.ds(n0 + cols0, cols0)],
        ext0.at[pl.ds(n0, cols0)],
        ext0.at[pl.ds(0, cols0)],
    )
    send_left(h0)
    send_right(h0)

    @pl.loop(1, rows0 - 1)
    def _(r):
        peer_row(r)

    for name in ("edge_self", "node_self", "node_message", "node_out"):
        loads[(name, 0)].wait()

    def node_part(rows, message, lv):
        pre = (
            mm(rows, node_self[lv])
            + mm(message, node_message[lv])
            + node_bias_ref[pl.ds(lv, 1), :]
        )
        hidden = gelu(pre).astype(BF)
        return (rows.astype(F32) + mm(hidden, node_out[lv])).astype(BF)

    base0 = me * n0 - cols0

    def fine_row(r):
        at = pl.multiple_of(r * cols0, cols0)
        rows = x[pl.ds(at, cols0), :]
        own = mm(rows, edge_self[0]) + edge_bias_ref[pl.ds(0, 1), :]
        ids = col0_ref[pl.ds(at, cols0), :] - (base0 + at)
        total = jnp.zeros((cols0, d), F32)
        for k in range(6):
            pick = onehot_cols(ids[:, k : k + 1], 3 * cols0)
            total = total + gelu(own + mm(pick, ext0[pl.ds(at, 3 * cols0), :]))
        fine[pl.ds(at, cols0), :] = node_part(rows, total.astype(BF), 0)

    @pl.loop(1, rows0 - 1)
    def _(r):
        fine_row(r)

    wait_left(h0)
    wait_right(h0)

    @pl.loop(0, 2)
    def _(i):
        fine_row(i * (rows0 - 1))

    half0 = n0 // 2
    q0 = par0_ref[...] - me * n1
    send1[0] = mm(onehot_rows(q0[:, :half0] + c1, c1), fine[pl.ds(0, half0), :]).astype(BF)
    send1[1] = mm(onehot_rows(q0[:, half0:] - n1, c1), fine[pl.ds(half0, half0), :]).astype(BF)
    h1 = halo(1, send1.at[0], recv1.at[1], send1.at[1], recv1.at[0])
    send_left(h1)
    send_right(h1)
    sums = mm(onehot_rows(q0, n1), fine[...])
    for name in ("edge_peer", "edge_self", "node_self", "node_message", "node_out"):
        loads[(name, 1)].wait()
    wait_left(h1)
    wait_right(h1)

    def normed(total, lv):
        scale = lax.rsqrt(jnp.mean(total * total, axis=1, keepdims=True) + 1e-05)
        return (total * scale * gain_ref[pl.ds(lv, 1), :]).astype(BF)

    first = sums[:c1] + recv1[0].astype(F32)
    last = sums[n1 - c1 :] + recv1[1].astype(F32)
    mid0 = normed(jnp.concatenate([first, last], axis=0), 0)

    ext1[pl.ds(c1, n1), :] = mm(mid0, edge_peer[1]).astype(BF)
    h2 = halo(
        2,
        ext1.at[pl.ds(c1, c1)],
        ext1.at[pl.ds(n1 + c1, c1)],
        ext1.at[pl.ds(n1, c1)],
        ext1.at[pl.ds(0, c1)],
    )
    send_left(h2)
    send_right(h2)
    own1 = mm(mid0, edge_self[1]) + edge_bias_ref[pl.ds(1, 1), :]
    ids1 = col1_ref[...] - (me * n1 - c1)
    wait_left(h2)
    wait_right(h2)
    total1 = jnp.zeros((n1, d), F32)
    for k in range(6):
        pick = onehot_cols(ids1[:, k : k + 1], n1 + 2 * c1)
        total1 = total1 + gelu(own1 + mm(pick, ext1[...]))
    mid[...] = node_part(mid0, total1.astype(BF), 1)

    q1 = par1_ref[...] - me * n2
    send2[0] = mm(onehot_rows(q1 + c2, c2), mid[...]).astype(BF)
    send2[1] = mm(onehot_rows(q1 - n2, c2), mid[...]).astype(BF)
    h3 = halo(3, send2.at[0], recv2.at[1], send2.at[1], recv2.at[0])
    send_left(h3)
    send_right(h3)
    sums2 = mm(onehot_rows(q1, n2), mid[...])
    for name in ("edge_peer", "edge_self", "node_self", "node_message", "node_out"):
        loads[(name, 2)].wait()
    wait_left(h3)
    wait_right(h3)
    coarse0 = normed(sums2 + recv2[0].astype(F32) + recv2[1].astype(F32), 1)

    def block(t):
        return gath.at[pl.ds(pl.multiple_of(t * n2, n2), n2)]

    gath[pl.ds(pl.multiple_of(me * n2, n2), n2), :] = mm(coarse0, edge_peer[2]).astype(BF)

    def forward(t, sem, to):
        return pltpu.make_async_remote_copy(
            src_ref=block(t),
            dst_ref=block(t),
            send_sem=sem,
            recv_sem=grecv.at[t],
            device_id={"tile": to},
        )

    started = []

    def go(t, sem, to):
        cp = forward(t, sem, to)
        cp.start()
        started.append(cp)

    mate_c = tile_of(zz, yy, c_other)
    for i, z in enumerate(z_partners):
        go(me, gsend_z.at[i], tile_of(z, yy, core))
    if span_y == 2:
        go(me, gsend_y.at[0], tile_of(zz, y_other, core))
    go(me, gsend_c.at[0], mate_c)

    for name in ("down_self", "down_parent", "down_out"):
        loads[name].wait()
    own2 = mm(coarse0, edge_self[2]) + edge_bias_ref[pl.ds(2, 1), :]

    def arrived(t):
        forward(t, gsend_c.at[0], mate_c).wait_recv()

    cslot = 1
    for i, z in enumerate(z_partners):
        t = tile_of(z, yy, core)
        arrived(t)
        if span_y == 2:
            go(t, gsend_y.at[i + 1], tile_of(zz, y_other, core))
        go(t, gsend_c.at[cslot], mate_c)
        cslot += 1

    if span_y == 2:
        for z in [zz] + z_partners:
            t = tile_of(z, y_other, core)
            arrived(t)
            go(t, gsend_c.at[cslot], mate_c)
            cslot += 1

    pre1[...] = mm(mid[...], down_self[1]) + down_bias_ref[pl.ds(1, 1), :]

    @pl.loop(0, rows0)
    def _(r):
        at = pl.multiple_of(r * cols0, cols0)
        pre0[pl.ds(at, cols0), :] = (
            mm(fine[pl.ds(at, cols0), :], down_self[0]) + down_bias_ref[pl.ds(0, 1), :]
        )

    ctab = ctab_ref[pl.ds(pl.multiple_of(me * n2, n2), n2), :]
    pick2 = jnp.concatenate(
        [onehot_cols(ctab[:, k : k + 1], gath.shape[0]) for k in range(6)], axis=0
    )
    for z in [zz] + z_partners:
        for y in [yy] + ([y_other] if span_y == 2 else []):
            arrived(tile_of(z, y, c_other))
    got = mm(pick2, gath[...])
    total2 = jnp.zeros((n2, d), F32)
    for k in range(6):
        total2 = total2 + gelu(own2 + got[k * n2 : (k + 1) * n2])
    coarse = node_part(coarse0, total2.astype(BF), 2)
    coarse_out[...] = coarse

    extc[pl.ds(c2, n2), :] = mm(coarse, down_parent[1]).astype(BF)
    h4 = halo(
        4,
        extc.at[pl.ds(c2, c2)],
        extc.at[pl.ds(n2 + c2, c2)],
        extc.at[pl.ds(n2, c2)],
        extc.at[pl.ds(0, c2)],
    )
    send_left(h4)
    send_right(h4)
    pick1 = onehot_cols(col1_ref[:, 6:7] - (me * n2 - c2), n2 + 2 * c2)
    wait_left(h4)
    wait_right(h4)
    hidden1 = gelu(pre1[...] + mm(pick1, extc[...])).astype(BF)
    mid_last = (mid[...].astype(F32) + mm(hidden1, down_out[1])).astype(BF)
    mid_out[...] = mid_last

    extl[pl.ds(c1, n1), :] = mm(mid_last, down_parent[0]).astype(BF)
    h5 = halo(
        5,
        extl.at[pl.ds(c1, c1)],
        extl.at[pl.ds(n1 + c1, c1)],
        extl.at[pl.ds(n1, c1)],
        extl.at[pl.ds(0, c1)],
    )
    send_left(h5)
    send_right(h5)
    wait_left(h5)
    wait_right(h5)

    @pl.loop(0, rows0)
    def _(r):
        at = pl.multiple_of(r * cols0, cols0)
        low = pl.multiple_of((r // 2) * c1, c1)
        pick = onehot_cols(col0_ref[pl.ds(at, cols0), 6:7] - (me * n1 - c1 + low), 3 * c1)
        lifted = mm(pick, extl[pl.ds(low, 3 * c1), :])
        hidden = gelu(pre0[pl.ds(at, cols0), :] + lifted).astype(BF)
        fine_out[pl.ds(at, cols0), :] = (
            fine[pl.ds(at, cols0), :].astype(F32) + mm(hidden, down_out[0])
        ).astype(BF)

    for h in (h0, h1, h2, h3, h4, h5):
        drain(h)
    for cp in started:
        cp.wait_send()


def local(
    n,
    span_y,
    fine_nodes,
    fine_table,
    mid_table,
    coarse_table,
    fine_parent,
    mid_parent,
    edge_self,
    edge_peer,
    edge_bias,
    node_self,
    node_message,
    node_bias,
    node_out,
    ascend_gain,
    down_self,
    down_parent,
    down_bias,
    down_out,
):
    n0, d = fine_nodes.shape
    n1 = mid_table.shape[0]
    n2 = coarse_table.shape[0] // n
    c1 = COLS // 2
    c2 = n2
    span_z = n // (2 * span_y)
    col0 = jnp.concatenate([fine_table, fine_parent[:, None]], axis=1)
    col1 = jnp.concatenate([mid_table, mid_parent[:, None]], axis=1)
    vm = pl.BlockSpec(memory_space=pltpu.VMEM)
    hbm = pl.BlockSpec(memory_space=pl.ANY)
    dma = pltpu.SemaphoreType.DMA
    return pl.pallas_call(
        functools.partial(sweep, n, span_y, COLS),
        out_shape=(
            jax.ShapeDtypeStruct((n0, d), BF),
            jax.ShapeDtypeStruct((n1, d), BF),
            jax.ShapeDtypeStruct((n2, d), BF),
        ),
        in_specs=[hbm] + [vm] * 5 + [hbm] * 8 + [vm] * 4,
        out_specs=(vm, vm, vm),
        scratch_shapes=[
            pltpu.VMEM((n0, d), BF),
            *[pltpu.VMEM((3, d, d), BF)] * 5,
            *[pltpu.VMEM((2, d, d), BF)] * 3,
            pltpu.VMEM((n0 + 2 * COLS, d), BF),
            pltpu.VMEM((n0, d), BF),
            pltpu.VMEM((n0, d), F32),
            pltpu.VMEM((2, c1, d), BF),
            pltpu.VMEM((2, c1, d), BF),
            pltpu.VMEM((n1 + 2 * c1, d), BF),
            pltpu.VMEM((n1, d), BF),
            pltpu.VMEM((n1, d), F32),
            pltpu.VMEM((2, c2, d), BF),
            pltpu.VMEM((2, c2, d), BF),
            pltpu.VMEM((n * n2, d), BF),
            pltpu.VMEM((n2 + 2 * c2, d), BF),
            pltpu.VMEM((n1 + 2 * c1, d), BF),
            dma((19,)),
            dma((12,)),
            dma((12,)),
            dma((max(span_z - 1, 1),)),
            dma((span_z,)),
            dma((n // 2,)),
            dma((n,)),
        ],
        compiler_params=pltpu.CompilerParams(
            collective_id=0, has_side_effects=True, vmem_limit_bytes=60 * 1024 * 1024
        ),
        name="sweep",
    )(
        fine_nodes,
        col0,
        col1,
        coarse_table,
        fine_parent[None, :],
        mid_parent[None, :],
        edge_self,
        edge_peer,
        node_self,
        node_message,
        node_out,
        down_self,
        down_parent,
        down_out,
        edge_bias,
        node_bias,
        ascend_gain,
        down_bias,
    )


def solution(mesh):
    n = mesh.shape["tile"]
    span_y = 2 if mesh.shape["groups"] == 2 else 1
    rep = P()
    return jax.shard_map(
        functools.partial(local, n, span_y),
        mesh=mesh,
        in_specs=(P(("groups", "tile"), None), P("tile", None), P("tile", None), rep, P("tile"), P("tile"))
        + (rep,) * 12,
        out_specs=(P(("groups", "tile"), None),) * 3,
        check_vma=False,
    )
```

```python
import functools

import jax
import jax.numpy as jnp
from jax import lax
from jax.experimental import pallas as pl
from jax.experimental.pallas import tpu as pltpu
from jax.sharding import PartitionSpec as P

COLS = 256
STACK = 3
VMEM_MIB = 63
BF = jnp.bfloat16
F32 = jnp.float32


def gelu(v):
    inner = v * (0.7978845608028654 + (0.7978845608028654 * 0.044715) * (v * v))
    half = 0.5 * v
    return half + half * jnp.tanh(inner)


def mm(a, b):
    return jnp.dot(a, b, preferred_element_type=F32)


def onehot_cols(ids, width):
    lanes = lax.broadcasted_iota(jnp.int32, (ids.shape[0], width), 1)
    return jnp.where(lanes == ids, 1.0, 0.0).astype(BF)


def onehot_rows(ids, height):
    rows = lax.broadcasted_iota(jnp.int32, (height, ids.shape[1]), 0)
    return jnp.where(rows == ids, 1.0, 0.0).astype(BF)


def sweep(
    n,
    span_y,
    cols0,
    x_hbm,
    tab0_ref,
    tab1_ref,
    ctab_ref,
    par0_ref,
    par1_ref,
    edge_self_hbm,
    edge_peer_hbm,
    node_self_hbm,
    node_message_hbm,
    node_out_hbm,
    down_self_hbm,
    down_parent_hbm,
    down_out_hbm,
    edge_bias_ref,
    node_bias_ref,
    gain_ref,
    down_bias_ref,
    fine_out,
    mid_out,
    coarse_out,
    x,
    edge_self,
    edge_peer,
    node_self,
    node_message,
    node_out,
    down_self,
    down_parent,
    down_out,
    ext0,
    fine,
    pre0,
    send1,
    recv1,
    ext1,
    mid,
    pre1,
    sums1,
    mid0,
    own1,
    pick2,
    send2,
    recv2,
    gath,
    extc,
    extl,
    col0_ref,
    col1_ref,
    ccol_ref,
    load_sem,
    send_sem,
    recv_sem,
    gsend_z,
    gsend_y,
    gsend_c,
    grecv,
):
    me = lax.axis_index("tile")
    n0, d = x.shape
    rows0 = n0 // cols0
    c1 = cols0 // 2
    n1 = mid.shape[0]
    n2 = coarse_out.shape[0]
    c2 = n2
    has_left = me > 0
    has_right = me < n - 1
    left = jnp.maximum(me - 1, 0)
    right = jnp.minimum(me + 1, n - 1)

    loads = {}
    slot = 0

    def load(name, src, dst):
        nonlocal slot
        cp = pltpu.make_async_copy(src, dst, load_sem.at[slot])
        cp.start()
        loads[name] = cp
        slot += 1

    load("x", x_hbm, x)
    load(("edge_peer", 0), edge_peer_hbm.at[0], edge_peer.at[0])
    load(("edge_self", 0), edge_self_hbm.at[0], edge_self.at[0])
    load(("node_self", 0), node_self_hbm.at[0], node_self.at[0])
    load(("node_message", 0), node_message_hbm.at[0], node_message.at[0])
    load(("node_out", 0), node_out_hbm.at[0], node_out.at[0])
    for lv in (1, 2):
        load(("edge_peer", lv), edge_peer_hbm.at[lv], edge_peer.at[lv])
        load(("edge_self", lv), edge_self_hbm.at[lv], edge_self.at[lv])
        load(("node_self", lv), node_self_hbm.at[lv], node_self.at[lv])
        load(("node_message", lv), node_message_hbm.at[lv], node_message.at[lv])
        load(("node_out", lv), node_out_hbm.at[lv], node_out.at[lv])
    load("down_self", down_self_hbm, down_self)
    load("down_parent", down_parent_hbm, down_parent)
    load("down_out", down_out_hbm, down_out)

    span_z = n // (2 * span_y)
    core = me % 2
    yy = (me // 2) % span_y
    zz = me // (2 * span_y)

    def tile_of(z, y, c):
        return (z * span_y + y) * 2 + c

    def zother(k):
        out = 0
        bit = 1
        while bit < span_z:
            mine = (zz // bit) % 2
            out = out + (1 - mine if k & bit else mine) * bit
            bit *= 2
        return out

    z_partners = [zother(k) for k in range(1, span_z)]
    y_other = 1 - yy if span_y == 2 else None
    c_other = 1 - core

    barrier = pltpu.get_barrier_semaphore()

    @pl.when(has_left)
    def _():
        pl.semaphore_signal(barrier, inc=1, device_id={"tile": left})

    @pl.when(has_right)
    def _():
        pl.semaphore_signal(barrier, inc=1, device_id={"tile": right})

    partners = [tile_of(z, yy, core) for z in z_partners]
    if span_y == 2:
        partners.append(tile_of(zz, y_other, core))
    partners.append(tile_of(zz, yy, c_other))
    for p in partners:
        pl.semaphore_signal(barrier, inc=1, device_id={"tile": p})

    def halo(e, low, low_dst, high, high_dst):
        to_left = pltpu.make_async_remote_copy(
            src_ref=low,
            dst_ref=low_dst,
            send_sem=send_sem.at[2 * e],
            recv_sem=recv_sem.at[2 * e + 1],
            device_id={"tile": left},
        )
        to_right = pltpu.make_async_remote_copy(
            src_ref=high,
            dst_ref=high_dst,
            send_sem=send_sem.at[2 * e + 1],
            recv_sem=recv_sem.at[2 * e],
            device_id={"tile": right},
        )
        return to_left, to_right

    def send_left(h):
        @pl.when(has_left)
        def _():
            h[0].start()

    def send_right(h):
        @pl.when(has_right)
        def _():
            h[1].start()

    def wait_left(h):
        @pl.when(has_left)
        def _():
            h[1].wait_recv()

    def wait_right(h):
        @pl.when(has_right)
        def _():
            h[0].wait_recv()

    left_far = core == 0

    def send_far(h):
        @pl.when(has_left & left_far)
        def _():
            h[0].start()

        @pl.when(has_right & (core == 1))
        def _():
            h[1].start()

    def send_near(h):
        @pl.when(has_left & (core == 1))
        def _():
            h[0].start()

        @pl.when(has_right & left_far)
        def _():
            h[1].start()

    def wait_far(h):
        @pl.when(has_left & left_far)
        def _():
            h[1].wait_recv()

        @pl.when(has_right & (core == 1))
        def _():
            h[0].wait_recv()

    def wait_near(h):
        @pl.when(has_left & (core == 1))
        def _():
            h[1].wait_recv()

        @pl.when(has_right & left_far)
        def _():
            h[0].wait_recv()

    def drain(h):
        @pl.when(has_left)
        def _():
            h[0].wait_send()

        @pl.when(has_right)
        def _():
            h[1].wait_send()

    def zero_edges(low, high):
        @pl.when(me == 0)
        def _():
            low[...] = jnp.zeros(low.shape, low.dtype)

        @pl.when(me == n - 1)
        def _():
            high[...] = jnp.zeros(high.shape, high.dtype)

    zero_edges(ext0.at[pl.ds(0, cols0)], ext0.at[pl.ds(n0 + cols0, cols0)])
    zero_edges(recv1.at[0], recv1.at[1])
    zero_edges(ext1.at[pl.ds(0, c1)], ext1.at[pl.ds(n1 + c1, c1)])
    zero_edges(recv2.at[0], recv2.at[1])
    zero_edges(extc.at[pl.ds(0, c2)], extc.at[pl.ds(n2 + c2, c2)])
    zero_edges(extl.at[pl.ds(0, c1)], extl.at[pl.ds(n1 + c1, c1)])

    def columns(tab_ref, par_ref, to):
        pad = jnp.zeros((1, tab_ref.shape[1]), jnp.int32)
        seventh = pad if par_ref is None else par_ref[...]
        to[...] = jnp.transpose(jnp.concatenate([tab_ref[...], seventh, pad], axis=0))

    columns(tab0_ref, par0_ref, col0_ref)
    columns(tab1_ref, par1_ref, col1_ref)
    columns(ctab_ref, None, ccol_ref)

    loads["x"].wait()
    loads[("edge_peer", 0)].wait()

    def peer_row(r):
        at = pl.multiple_of(r * cols0, cols0)
        ext0[pl.ds(pl.multiple_of(at + cols0, cols0), cols0), :] = mm(
            x[pl.ds(at, cols0), :], edge_peer[0]
        ).astype(BF)

    peer_row(0)
    peer_row(rows0 - 1)
    pl.semaphore_wait(barrier, len(partners) + has_left.astype(jnp.int32) + has_right.astype(jnp.int32))
    h0 = halo(
        0,
        ext0.at[pl.ds(cols0, cols0)],
        ext0.at[pl.ds(n0 + cols0, cols0)],
        ext0.at[pl.ds(n0, cols0)],
        ext0.at[pl.ds(0, cols0)],
    )
    send_left(h0)
    send_right(h0)

    @pl.loop(1, rows0 - 1)
    def _(r):
        peer_row(r)

    for name in ("edge_self", "node_self", "node_message", "node_out"):
        loads[(name, 0)].wait()

    def node_part(rows, message, lv):
        pre = (
            mm(rows, node_self[lv])
            + mm(message, node_message[lv])
            + node_bias_ref[pl.ds(lv, 1), :]
        )
        hidden = gelu(pre).astype(BF)
        return (rows.astype(F32) + mm(hidden, node_out[lv])).astype(BF)

    base0 = me * n0 - cols0

    def fine_row(r):
        at = pl.multiple_of(r * cols0, cols0)
        rows = x[pl.ds(at, cols0), :]
        own = mm(rows, edge_self[0]) + edge_bias_ref[pl.ds(0, 1), :]
        ids = col0_ref[pl.ds(at, cols0), :] - (base0 + at)
        total = jnp.zeros((cols0, d), F32)
        for k in range(0, 6, STACK):
            picks = [onehot_cols(ids[:, k + j : k + j + 1], 3 * cols0) for j in range(STACK)]
            got = mm(jnp.concatenate(picks, axis=0), ext0[pl.ds(at, 3 * cols0), :])
            for j in range(STACK):
                total = total + gelu(own + got[j * cols0 : (j + 1) * cols0])
        fine[pl.ds(at, cols0), :] = node_part(rows, total.astype(BF), 0)

    @pl.loop(1, rows0 - 1)
    def _(r):
        fine_row(r)

    half0 = n0 // 2
    wait_left(h0)
    wait_right(h0)
    h1 = halo(1, send1.at[0], recv1.at[1], send1.at[1], recv1.at[0])

    def edge(side):
        fine_row(side * (rows0 - 1))
        at = pl.multiple_of(side * half0, half0)
        q = par0_ref[:, pl.ds(at, half0)] - (me * n1 - c1 + side * (n1 + c1))
        send1[side] = mm(onehot_rows(q, c1), fine[pl.ds(at, half0), :]).astype(BF)

    @pl.loop(0, 2)
    def _(i):
        far = i == 0
        edge((1 - i) * core + i * (1 - core))

        @pl.when(far)
        def _():
            send_far(h1)

        @pl.when(i == 1)
        def _():
            send_near(h1)

    sums1[...] = mm(onehot_rows(par0_ref[...] - me * n1, n1), fine[...])
    for name in ("edge_peer", "edge_self", "node_self", "node_message", "node_out"):
        loads[(name, 1)].wait()

    def normed(total, lv):
        scale = lax.rsqrt(jnp.mean(total * total, axis=1, keepdims=True) + 1e-05)
        return (total * scale * gain_ref[pl.ds(lv, 1), :]).astype(BF)

    h2 = halo(
        2,
        ext1.at[pl.ds(c1, c1)],
        ext1.at[pl.ds(n1 + c1, c1)],
        ext1.at[pl.ds(n1, c1)],
        ext1.at[pl.ds(0, c1)],
    )

    def mid_start(side):
        at = pl.multiple_of(side * c1, c1)
        rows = normed(sums1[pl.ds(at, c1), :] + recv1[side].astype(F32), 0)
        mid0[pl.ds(at, c1), :] = rows
        ext1[pl.ds(pl.multiple_of(at + c1, c1), c1), :] = mm(rows, edge_peer[1]).astype(BF)

    wait_near(h1)
    mid_start(1 - core)
    send_near(h2)
    wait_far(h1)
    mid_start(core)
    send_far(h2)
    own1[...] = mm(mid0[...], edge_self[1]) + edge_bias_ref[pl.ds(1, 1), :]

    def mid_row(side):
        at = pl.multiple_of(side * c1, c1)
        rows = mid0[pl.ds(at, c1), :]
        own = own1[pl.ds(at, c1), :]
        ids = col1_ref[pl.ds(at, c1), :] - (me * n1 - c1 + at)
        picks = jnp.concatenate([onehot_cols(ids[:, k : k + 1], 3 * c1) for k in range(6)], axis=0)
        got = mm(picks, ext1[pl.ds(at, 3 * c1), :])
        total = jnp.zeros((c1, d), F32)
        for k in range(6):
            total = total + gelu(own + got[k * c1 : (k + 1) * c1])
        mid[pl.ds(at, c1), :] = node_part(rows, total.astype(BF), 1)

    @pl.loop(0, 2)
    def _(i):
        @pl.when(i == 0)
        def _():
            wait_near(h2)

        @pl.when(i == 1)
        def _():
            wait_far(h2)

        mid_row((1 - i) * (1 - core) + i * core)

    q1 = par1_ref[...] - me * n2
    send2[0] = mm(onehot_rows(q1 + c2, c2), mid[...]).astype(BF)
    send2[1] = mm(onehot_rows(q1 - n2, c2), mid[...]).astype(BF)
    h3 = halo(3, send2.at[0], recv2.at[1], send2.at[1], recv2.at[0])
    send_left(h3)
    send_right(h3)
    sums2 = mm(onehot_rows(q1, n2), mid[...])
    for name in ("edge_peer", "edge_self", "node_self", "node_message", "node_out"):
        loads[(name, 2)].wait()
    wait_left(h3)
    wait_right(h3)
    coarse0 = normed(sums2 + recv2[0].astype(F32) + recv2[1].astype(F32), 1)

    def block(t):
        return gath.at[pl.ds(pl.multiple_of(t * n2, n2), n2)]

    gath[pl.ds(pl.multiple_of(me * n2, n2), n2), :] = mm(coarse0, edge_peer[2]).astype(BF)

    def forward(t, sem, to):
        return pltpu.make_async_remote_copy(
            src_ref=block(t),
            dst_ref=block(t),
            send_sem=sem,
            recv_sem=grecv.at[t],
            device_id={"tile": to},
        )

    started = []

    def go(t, sem, to):
        cp = forward(t, sem, to)
        cp.start()
        started.append(cp)

    mate_c = tile_of(zz, yy, c_other)
    for i, z in enumerate(z_partners):
        go(me, gsend_z.at[i], tile_of(z, yy, core))
    if span_y == 2:
        go(me, gsend_y.at[0], tile_of(zz, y_other, core))
    go(me, gsend_c.at[0], mate_c)

    for name in ("down_self", "down_parent", "down_out"):
        loads[name].wait()
    own2 = mm(coarse0, edge_self[2]) + edge_bias_ref[pl.ds(2, 1), :]

    def arrived(t):
        forward(t, gsend_c.at[0], mate_c).wait_recv()

    def pre_row(r):
        at = pl.multiple_of(r * cols0, cols0)
        pre0[pl.ds(at, cols0), :] = (
            mm(fine[pl.ds(at, cols0), :], down_self[0]) + down_bias_ref[pl.ds(0, 1), :]
        )

    def pre_mid(_):
        pre1[...] = mm(mid[...], down_self[1]) + down_bias_ref[pl.ds(1, 1), :]

    work = [functools.partial(pre_row, r) for r in range(rows0)]
    work.append(functools.partial(pre_mid, 0))

    ctab = ccol_ref[pl.ds(pl.multiple_of(me * n2, n2), n2), :]
    for k in range(6):
        pick2[pl.ds(k * n2, n2), :] = onehot_cols(ctab[:, k : k + 1], gath.shape[0])

    cslot = 1
    for i, z in enumerate(z_partners):
        t = tile_of(z, yy, core)
        arrived(t)
        if span_y == 2:
            go(t, gsend_y.at[i + 1], tile_of(zz, y_other, core))
        go(t, gsend_c.at[cslot], mate_c)
        cslot += 1
        if work:
            work.pop(0)()

    if span_y == 2:
        for z in [zz] + z_partners:
            t = tile_of(z, y_other, core)
            arrived(t)
            go(t, gsend_c.at[cslot], mate_c)
            cslot += 1
            if work:
                work.pop(0)()
    for job in work:
        job()

    for z in [zz] + z_partners:
        for y in [yy] + ([y_other] if span_y == 2 else []):
            arrived(tile_of(z, y, c_other))
    got = mm(pick2[...], gath[...])
    total2 = jnp.zeros((n2, d), F32)
    for k in range(6):
        total2 = total2 + gelu(own2 + got[k * n2 : (k + 1) * n2])
    coarse = node_part(coarse0, total2.astype(BF), 2)
    coarse_out[...] = coarse

    extc[pl.ds(c2, n2), :] = mm(coarse, down_parent[1]).astype(BF)
    h4 = halo(
        4,
        extc.at[pl.ds(c2, c2)],
        extc.at[pl.ds(n2 + c2, c2)],
        extc.at[pl.ds(n2, c2)],
        extc.at[pl.ds(0, c2)],
    )
    send_left(h4)
    send_right(h4)
    pick1 = onehot_cols(col1_ref[:, 6:7] - (me * n2 - c2), n2 + 2 * c2)
    wait_left(h4)
    wait_right(h4)
    hidden1 = gelu(pre1[...] + mm(pick1, extc[...])).astype(BF)
    mid_last = (mid[...].astype(F32) + mm(hidden1, down_out[1])).astype(BF)
    mid_out[...] = mid_last

    extl[pl.ds(c1, n1), :] = mm(mid_last, down_parent[0]).astype(BF)
    h5 = halo(
        5,
        extl.at[pl.ds(c1, c1)],
        extl.at[pl.ds(n1 + c1, c1)],
        extl.at[pl.ds(n1, c1)],
        extl.at[pl.ds(0, c1)],
    )
    send_far(h5)
    send_near(h5)

    def last_row(r):
        at = pl.multiple_of(r * cols0, cols0)
        low = pl.multiple_of((r // 2) * c1, c1)
        pick = onehot_cols(col0_ref[pl.ds(at, cols0), 6:7] - (me * n1 - c1 + low), 3 * c1)
        lifted = mm(pick, extl[pl.ds(low, 3 * c1), :])
        hidden = gelu(pre0[pl.ds(at, cols0), :] + lifted).astype(BF)
        fine_out[pl.ds(at, cols0), :] = (
            fine[pl.ds(at, cols0), :].astype(F32) + mm(hidden, down_out[0])
        ).astype(BF)

    @pl.loop(0, rows0)
    def _(i):
        @pl.when(i == 0)
        def _():
            wait_near(h5)

        @pl.when(i == rows0 // 2)
        def _():
            wait_far(h5)

        later = i // (rows0 // 2)
        side = (1 - later) * (1 - core) + later * core
        last_row(i % (rows0 // 2) + side * (rows0 // 2))

    for h in (h0, h1, h2, h3, h4, h5):
        drain(h)
    for cp in started:
        cp.wait_send()


def local(
    n,
    span_y,
    fine_nodes,
    fine_table,
    mid_table,
    coarse_table,
    fine_parent,
    mid_parent,
    edge_self,
    edge_peer,
    edge_bias,
    node_self,
    node_message,
    node_bias,
    node_out,
    ascend_gain,
    down_self,
    down_parent,
    down_bias,
    down_out,
):
    n0, d = fine_nodes.shape
    n1 = mid_table.shape[0]
    n2 = coarse_table.shape[0] // n
    c1 = COLS // 2
    c2 = n2
    span_z = n // (2 * span_y)
    vm = pl.BlockSpec(memory_space=pltpu.VMEM)
    hbm = pl.BlockSpec(memory_space=pltpu.HBM)
    dma = pltpu.SemaphoreType.DMA
    return pl.pallas_call(
        functools.partial(sweep, n, span_y, COLS),
        out_shape=(
            jax.ShapeDtypeStruct((n0, d), BF),
            jax.ShapeDtypeStruct((n1, d), BF),
            jax.ShapeDtypeStruct((n2, d), BF),
        ),
        in_specs=[hbm] + [vm] * 5 + [hbm] * 8 + [vm] * 4,
        out_specs=(vm, vm, vm),
        scratch_shapes=[
            pltpu.VMEM((n0, d), BF),
            *[pltpu.VMEM((3, d, d), BF)] * 5,
            *[pltpu.VMEM((2, d, d), BF)] * 3,
            pltpu.VMEM((n0 + 2 * COLS, d), BF),
            pltpu.VMEM((n0, d), BF),
            pltpu.VMEM((n0, d), F32),
            pltpu.VMEM((2, c1, d), BF),
            pltpu.VMEM((2, c1, d), BF),
            pltpu.VMEM((n1 + 2 * c1, d), BF),
            pltpu.VMEM((n1, d), BF),
            pltpu.VMEM((n1, d), F32),
            pltpu.VMEM((n1, d), F32),
            pltpu.VMEM((n1, d), BF),
            pltpu.VMEM((n1, d), F32),
            pltpu.VMEM((6 * n2, n * n2), BF),
            pltpu.VMEM((2, c2, d), BF),
            pltpu.VMEM((2, c2, d), BF),
            pltpu.VMEM((n * n2, d), BF),
            pltpu.VMEM((n2 + 2 * c2, d), BF),
            pltpu.VMEM((n1 + 2 * c1, d), BF),
            pltpu.VMEM((n0, 8), jnp.int32),
            pltpu.VMEM((n1, 8), jnp.int32),
            pltpu.VMEM((n * n2, 8), jnp.int32),
            dma((21,)),
            dma((12,)),
            dma((12,)),
            dma((max(span_z - 1, 1),)),
            dma((span_z,)),
            dma((n // 2,)),
            dma((n,)),
        ],
        compiler_params=pltpu.CompilerParams(
            collective_id=0, has_side_effects=True, vmem_limit_bytes=VMEM_MIB * 1024 * 1024
        ),
        name="sweep",
    )(
        fine_nodes,
        fine_table.T,
        mid_table.T,
        coarse_table.T,
        fine_parent[None, :],
        mid_parent[None, :],
        edge_self,
        edge_peer,
        node_self,
        node_message,
        node_out,
        down_self,
        down_parent,
        down_out,
        edge_bias,
        node_bias,
        ascend_gain,
        down_bias,
    )


def solution(mesh):
    n = mesh.shape["tile"]
    span_y = 2 if mesh.shape["groups"] == 2 else 1
    rep = P()
    return jax.shard_map(
        functools.partial(local, n, span_y),
        mesh=mesh,
        in_specs=(P(("groups", "tile"), None), P("tile", None), P("tile", None), rep, P("tile"), P("tile"))
        + (rep,) * 12,
        out_specs=(P(("groups", "tile"), None),) * 3,
        check_vma=False,
    )
```
